32 devices in a mesh: groups: 2 (over x), expert: 2 (over core), seq: 8 (over z, y).
Axes of the slice: x: 2, y: 2, z: 4, core: 2. Of those that a mesh axis runs over, the one named last changes fastest.
Arguments:
- query_heads: bfloat16 [2, 2, 2080, 4096], P('expert', 'groups', 'seq'), parts along dimension 1, may hold values from -100 to 100
- key_heads: bfloat16 [2, 2, 2080, 4096], P('expert', 'groups', 'seq'), parts along dimension 1, may hold values from -8 to 8
- value_heads: bfloat16 [2, 2, 2080, 4096], P('expert', 'groups', 'seq'), parts along dimension 1, may hold values from -6 to 6
- residual: bfloat16 [2, 2, 2080, 5120], P('expert', 'groups', 'seq'), parts along dimension 1, may hold values from -6 to 6
- out_weight: bfloat16 [2, 4096, 5120], P('expert', 'seq'), may hold values from -0.09375 to 0.09375
- mod_weight: bfloat16 [2, 256, 15360], P('expert'), may hold values from -0.375 to 0.375
- head_weight: bfloat16 [2, 5120, 64], P('expert'), may hold values from -0.078125 to 0.078125
- latent: float32 [2, 2080, 64], P('groups', 'seq'), parts along dimension 0, may hold values from -6 to 6
- timesteps: int32 [2, 2], P('expert', 'groups'), parts along dimension 1, may hold values from 26 to 1000, as said below
- token_order: int32 [2, 2, 2080], P(None, 'groups'), parts along dimension 1, may hold values from 0 to 2079, as said below
Outputs:
- velocity: float32 [2, 2, 2080, 64], P('expert', 'groups', 'seq'), parts along dimension 1
- latents_out: float32 [2, 2, 2080, 64], P('expert', 'groups', 'seq'), parts along dimension 1
The draws below stay inside these ranges and needn't reach their ends.
There are 2 independent parts, one for each index of `groups`. The reference program is written for one: setup_inputs(seed, part) draws one part's arguments, and reference() takes and returns one part's arrays. A program takes and returns all parts, laid end to end along the dimension named above; an argument that names none is the same for every part. Nothing has to cross between parts.
Inputs may be any that keep to these rules, and one draw needn't show every extreme that they name: Each token_order[e, m] is a permutation of 0 to 2079. timesteps[0, m] is at least 876 and timesteps[1, m] at most 875.
All inputs are finite; a program needn't handle non-finite values.
Results may differ from the reference program's by a relative error of at most 0.0085.
Values may be sent and summed in bfloat16 or wider, within the bound.
A program may use at most 192 MiB of HBM per device.

```python
import jax
import jax.numpy as jnp
from jax import lax

D = 5120
HEAD_DIM = 128
FREQ = 256
LATENT = 64
HEADS = 32
HGRID = 20
WGRID = 52
MB = 1
STRIDE = 25
L = 2080


def token_orders(key):
    streams = jax.random.split(jax.random.fold_in(key, 4099), 2 * MB)
    shuffled = jax.vmap(lambda stream: jax.random.permutation(stream, L))(streams)
    return shuffled.reshape(2, MB, L).astype(jnp.int32)


def drawn_fields(key):
    first_key, second_key = jax.random.split(jax.random.fold_in(key, 5003))
    field_shape = (2, MB, L, HEADS, HEAD_DIM)
    queries = jnp.clip(jax.random.normal(first_key, field_shape), -4.0, 4.0)
    keys_out = jnp.clip(jax.random.normal(second_key, field_shape), -4.0, 4.0)
    return (queries, keys_out)


def draw_query_heads(key, part):
    return drawn_fields(key)[0].reshape(2, MB, L, HEADS * HEAD_DIM).astype(jnp.bfloat16)


def draw_key_heads(key, part):
    return drawn_fields(key)[1].reshape(2, MB, L, HEADS * HEAD_DIM).astype(jnp.bfloat16)


def draw_residual(key, part):
    split_keys = jax.random.split(jax.random.fold_in(key, 9001), 1)
    field = 0.03 * jax.random.normal(split_keys[0], (2, MB, L, D))
    return field.astype(jnp.bfloat16)


def draw_timesteps(key, part):
    early_key, late_key = jax.random.split(jax.random.fold_in(key, 8191))
    upper_steps = jax.random.randint(early_key, (1, MB), 876, 1001)
    lower_steps = jax.random.randint(late_key, (1, MB), 26, 876)
    return jnp.concatenate([upper_steps, lower_steps], axis=0).astype(jnp.int32)


def draw_token_order(key, part):
    return token_orders(key)


def shard_levels(stream_key, extent, shards, least, top_value):
    gain, own = 1.0, jax.random.fold_in(stream_key, 6)
    for position, shards_of in shards:
        steps = jnp.exp(jax.random.uniform(jax.random.fold_in(own, position), (shards_of,), jnp.float32, least / len(shards), top_value / len(shards)))
        gain = gain * jnp.repeat(steps, extent[position] // shards_of).reshape([-1 if axis == position else 1 for axis in range(len(extent))])
    return gain


def noise(own_key, dims, width, limit, cuts=(), held_as=jnp.bfloat16):
    level = shard_levels(own_key, dims, cuts, -0.22, 0.18) if cuts else 1.0
    entries = jax.random.normal(own_key, dims, jnp.float32) * width * level
    return jnp.minimum(jnp.maximum(entries, -limit), limit).astype(held_as)


def setup_inputs(seed: int = 0, part: int = 0) -> dict:
    seeds = jax.random.split(jax.random.key(seed), 11)
    own_keys = jax.random.split(jax.random.fold_in(seeds[10], part), 11)
    query_heads = draw_query_heads(jax.random.fold_in(jax.random.fold_in(seeds[10], part), 71), part)
    key_heads = draw_key_heads(jax.random.fold_in(jax.random.fold_in(seeds[10], part), 71), part)
    value_heads = noise(own_keys[2], (2, MB, L, HEADS * HEAD_DIM), 1.0, 6.0, ((0, 2), (2, 8)))
    residual = draw_residual(jax.random.fold_in(jax.random.fold_in(seeds[10], part), 71), part)
    out_weight = noise(seeds[4], (2, HEADS * HEAD_DIM, D), (HEADS * HEAD_DIM) ** -0.5, 0.09375, ((0, 2), (1, 8)))
    mod_weight = noise(seeds[5], (2, FREQ, 3 * D), FREQ ** -0.5, 0.375, ((0, 2),))
    head_weight = noise(seeds[6], (2, D, LATENT), D ** -0.5, 0.078125, ((0, 2),))
    latent = noise(own_keys[7], (MB, L, LATENT), 1.0, 6.0, ((1, 8),), jnp.float32)
    timesteps = draw_timesteps(jax.random.fold_in(jax.random.fold_in(seeds[10], part), 71), part)
    token_order = draw_token_order(jax.random.fold_in(jax.random.fold_in(seeds[10], part), 71), part)
    return dict(query_heads=query_heads, key_heads=key_heads, value_heads=value_heads, residual=residual, out_weight=out_weight, mod_weight=mod_weight, head_weight=head_weight, latent=latent, timesteps=timesteps, token_order=token_order)


flow_shift = 5.0
norm_eps = 1e-06

def ladder(length):
    return 10000.0 ** (-jnp.arange(length, dtype=jnp.float32) / length)

def rope_angles(tokens):
    half_dim = HEAD_DIM // 2
    side_pairs = half_dim // 3
    frame_pairs = half_dim - 2 * side_pairs
    frame_pos = (tokens // (HGRID * WGRID)).astype(jnp.float32)
    row_pos = (tokens // WGRID % HGRID).astype(jnp.float32)
    column_pos = (tokens % WGRID).astype(jnp.float32)
    return jnp.concatenate([frame_pos[:, None] * ladder(frame_pairs), row_pos[:, None] * ladder(side_pairs), column_pos[:, None] * ladder(side_pairs)], axis=1)

def rotate(field, angles):
    row_count = field.shape[0]
    paired = field.reshape(row_count, -1, HEAD_DIM // 2, 2)
    cosine = jnp.cos(angles)[:, None, :]
    sine_part = jnp.sin(angles)[:, None, :]
    even_part = paired[..., 0]
    odd_part = paired[..., 1]
    turned = jnp.stack([even_part * cosine - odd_part * sine_part, even_part * sine_part + odd_part * cosine], axis=-1)
    return turned.reshape(row_count, -1)

def stamp_embedding(step_value):
    half_freq = FREQ // 2
    inverse_rates = 10000.0 ** (-jnp.arange(half_freq, dtype=jnp.float32) / half_freq)
    phases = step_value * inverse_rates
    return jnp.concatenate([jnp.cos(phases), jnp.sin(phases)])

def noise_level(step_value):
    scaled = step_value / 1000.0
    return flow_shift * scaled / (1.0 + (flow_shift - 1.0) * scaled)

def attend(turned_q, turned_k, values_in):
    split_q = turned_q.reshape(L, HEADS, HEAD_DIM).transpose(1, 0, 2)
    split_k = turned_k.reshape(L, HEADS, HEAD_DIM).transpose(1, 0, 2)
    split_v = values_in.reshape(L, HEADS, HEAD_DIM).transpose(1, 0, 2)

    def one_head(operands):
        head_q, head_k, head_v = operands
        scores = jnp.dot(head_q, head_k.T, preferred_element_type=jnp.float32) * HEAD_DIM ** (-0.5)
        row_max = lax.optimization_barrier(jnp.max(scores, axis=1, keepdims=True))
        weights = jnp.exp(scores - row_max)
        row_total = lax.optimization_barrier(jnp.sum(weights, axis=1, keepdims=True))
        mixed = jnp.dot(weights.astype(jnp.bfloat16), head_v, preferred_element_type=jnp.float32)
        return (mixed / row_total).astype(jnp.bfloat16)
    heads_out = lax.map(one_head, (split_q, split_k, split_v))
    return heads_out.transpose(1, 0, 2).reshape(L, HEADS * HEAD_DIM)

def expert_velocity(queries, keys_in, values_in, residual_rows, out_w, mod_w, head_w, order, step_value):
    angles = rope_angles(order)
    turned_q = rotate(queries.astype(jnp.float32), angles).astype(jnp.bfloat16)
    turned_k = rotate(keys_in.astype(jnp.float32), angles).astype(jnp.bfloat16)
    mixed = attend(turned_q, turned_k, values_in)
    projection = jnp.dot(mixed, out_w, preferred_element_type=jnp.float32)
    embedded = stamp_embedding(step_value).astype(jnp.bfloat16)
    modulation = jnp.dot(embedded[None], mod_w, preferred_element_type=jnp.float32)[0]
    gate_vec = modulation[:D]
    shift_vec = modulation[D:2 * D]
    scale_vec = modulation[2 * D:]
    hidden = residual_rows.astype(jnp.float32) + gate_vec * projection
    centered = hidden - lax.optimization_barrier(jnp.mean(hidden, axis=1, keepdims=True))
    variance = lax.optimization_barrier(jnp.mean(centered * centered, axis=1, keepdims=True))
    normed = (centered * lax.rsqrt(variance + norm_eps) * (1.0 + scale_vec) + shift_vec).astype(jnp.bfloat16)
    return jnp.dot(normed, head_w, preferred_element_type=jnp.float32)

def reference(query_heads, key_heads, value_heads, residual, out_weight, mod_weight, head_weight, latent, timesteps, token_order):
    high_speed, low_speed, high_latent, low_latent = ([], [], [], [])
    for micro_no in range(MB):
        speeds = []
        changes = []
        for expert_no in range(2):
            step_value = timesteps[expert_no, micro_no].astype(jnp.float32)
            speeds.append(expert_velocity(query_heads[expert_no, micro_no], key_heads[expert_no, micro_no], value_heads[expert_no, micro_no], residual[expert_no, micro_no], out_weight[expert_no], mod_weight[expert_no], head_weight[expert_no], token_order[expert_no, micro_no], step_value))
            changes.append(noise_level(step_value - STRIDE) - noise_level(step_value))
        stepped = latent[micro_no] + changes[0] * speeds[0]
        first_order = token_order[0, micro_no]
        inverse = jnp.zeros((L,), jnp.int32).at[first_order].set(jnp.arange(L, dtype=jnp.int32))
        started = stepped[inverse[token_order[1, micro_no]]]
        high_speed.append(speeds[0])
        low_speed.append(speeds[1])
        high_latent.append(stepped)
        low_latent.append(started + changes[1] * speeds[1])
    velocity = jnp.stack([jnp.stack(high_speed), jnp.stack(low_speed)])
    latents_out = jnp.stack([jnp.stack(high_latent), jnp.stack(low_latent)])
    return (velocity, latents_out)
```

```python
import jax
import jax.numpy as jnp
from jax import lax
from jax.experimental import pallas as pl
from jax.experimental.pallas import tpu as pltpu
from jax.sharding import PartitionSpec as P

HEAD_DIM = 128
FREQ = 256
HGRID = 20
WGRID = 52
STRIDE = 25


flow_shift = 5.0
norm_eps = 1e-06

DEGREE = 4
CHUNKS = 2
COLUMN_CHUNKS = 4
LOG2E = 1.4426950408889634


def ladder(length):
    return 10000.0 ** (-jnp.arange(length, dtype=jnp.float32) / length)


def rope_angles(tokens):
    half_dim = HEAD_DIM // 2
    side_pairs = half_dim // 3
    frame_pairs = half_dim - 2 * side_pairs
    frame_pos = (tokens // (HGRID * WGRID)).astype(jnp.float32)
    row_pos = (tokens // WGRID % HGRID).astype(jnp.float32)
    column_pos = (tokens % WGRID).astype(jnp.float32)
    return jnp.concatenate(
        [
            frame_pos[:, None] * ladder(frame_pairs),
            row_pos[:, None] * ladder(side_pairs),
            column_pos[:, None] * ladder(side_pairs),
        ],
        axis=1,
    )


def stamp_embedding(step_value):
    half_freq = FREQ // 2
    inverse_rates = 10000.0 ** (-jnp.arange(half_freq, dtype=jnp.float32) / half_freq)
    phases = step_value * inverse_rates
    return jnp.concatenate([jnp.cos(phases), jnp.sin(phases)])


def noise_level(step_value):
    scaled = step_value / 1000.0
    return flow_shift * scaled / (1.0 + (flow_shift - 1.0) * scaled)


def swap(value, axis, flip):
    return lax.ppermute(value, axis, [(i, i ^ flip) for i in range(lax.axis_size(axis))])


def turn_kernel(place_ref, q_ref, k_ref, v_ref, cos_ref, next_ref, prev_ref, out_ref):
    cosine = cos_ref[...]
    from_next = next_ref[...]
    from_prev = prev_ref[...]

    def turned(field):
        ahead = pltpu.roll(field, HEAD_DIM - 1, 1)
        behind = pltpu.roll(field, 1, 1)
        return field * cosine + ahead * from_next + behind * from_prev

    for head in range(q_ref.shape[1] // HEAD_DIM):
        cols = pl.ds(head * HEAD_DIM, HEAD_DIM)
        out_ref[0, :, cols] = turned(k_ref[:, cols].astype(jnp.float32)).astype(jnp.bfloat16)
        turned_q = turned(q_ref[:, cols].astype(jnp.float32)) * (LOG2E * HEAD_DIM**-0.5)
        out_ref[2, :, cols] = turned_q.astype(jnp.bfloat16)
    out_ref[1] = v_ref[...]


def turn(place, queries, keys, values, tables, flip, chunk, width):
    rows = queries.shape[0]
    pick = lambda i, place_ref: (0, (place_ref[0] ^ flip) * CHUNKS + chunk)
    fixed = lambda i, place_ref: (0, 0)
    return pl.pallas_call(
        turn_kernel,
        grid_spec=pltpu.PrefetchScalarGridSpec(
            num_scalar_prefetch=1,
            grid=(1,),
            in_specs=[pl.BlockSpec((rows, width), pick)] * 3
            + [pl.BlockSpec((rows, HEAD_DIM), fixed)] * 3,
            out_specs=pl.BlockSpec((3, rows, width), lambda i, place_ref: (0, 0, 0)),
        ),
        out_shape=jax.ShapeDtypeStruct((3, rows, width), jnp.bfloat16),
        cost_estimate=pl.CostEstimate(
            flops=20 * rows * width, bytes_accessed=12 * rows * width, transcendentals=0
        ),
        name="turn",
    )(place, queries, keys, values, *tables)


def attend_kernel(near_count, far_count, padded, *refs):
    near = refs[:near_count]
    far = refs[near_count : near_count + far_count]
    out_ref, k_scr, v_scr = refs[near_count + far_count :]
    rows = near[0].shape[1]

    @pl.when(pl.program_id(0) == 0)
    def _():
        k_scr[...] = jnp.zeros_like(k_scr)
        v_scr[...] = jnp.zeros_like(v_scr)

    for slot, block in enumerate(near + far):
        k_scr[pl.ds(slot * padded, rows), :] = block[0]
        v_scr[pl.ds(slot * padded, rows), :] = block[1]
    spot = lax.broadcasted_iota(jnp.int32, (1, k_scr.shape[0]), 1) % padded
    hide = jnp.where(spot < rows, 0.0, -1e30).astype(jnp.float32)
    for slot, block in enumerate(near):
        scores = (
            lax.dot_general(
                block[2], k_scr[...], (((1,), (1,)), ((), ())), preferred_element_type=jnp.float32
            )
            + hide
        )
        top = jnp.max(scores, axis=1, keepdims=True)
        weights = jnp.exp2(scores - top)
        total = jnp.sum(weights, axis=1, keepdims=True)
        mixed = jnp.dot(
            weights.astype(jnp.bfloat16), v_scr[...], preferred_element_type=jnp.float32
        )
        out_ref[slot] = (mixed / total).astype(jnp.bfloat16)


def attend(near, far):
    rows, width = near[0].shape[1:]
    padded = -(-rows // 16) * 16
    blocks = len(near) + len(far)
    keys = blocks * padded
    work = len(near) * rows * keys * width
    return pl.pallas_call(
        lambda *refs: attend_kernel(len(near), len(far), padded, *refs),
        grid=(width // HEAD_DIM,),
        in_specs=[pl.BlockSpec((3, rows, HEAD_DIM), lambda h: (0, 0, h))] * len(near)
        + [pl.BlockSpec((2, rows, HEAD_DIM), lambda h: (0, 0, h))] * len(far),
        out_specs=pl.BlockSpec((len(near), rows, HEAD_DIM), lambda h: (0, 0, h)),
        out_shape=jax.ShapeDtypeStruct((len(near), rows, width), jnp.bfloat16),
        scratch_shapes=[pltpu.VMEM((keys, HEAD_DIM), jnp.bfloat16)] * 2,
        cost_estimate=pl.CostEstimate(
            flops=4 * work, bytes_accessed=8 * blocks * rows * width, transcendentals=work // HEAD_DIM
        ),
        name="attend",
    )(*near, *far)


def project_kernel(count, *refs):
    out_ref = refs[-1]
    total = jnp.dot(refs[0][...], refs[count][...], preferred_element_type=jnp.float32)
    for part in range(1, count):
        total += jnp.dot(refs[part][...], refs[count + part][...], preferred_element_type=jnp.float32)
    out_ref[...] = total.astype(out_ref.dtype)


def project(slot, chunk, lefts, rights, dtype):
    rows = lefts[0].shape[1]
    columns = rights[0].shape[1] // COLUMN_CHUNKS
    tile = 256
    tiles = columns // tile
    depth = sum(left.shape[2] for left in lefts)
    return pl.pallas_call(
        lambda *refs: project_kernel(len(lefts), *refs),
        grid=(tiles,),
        in_specs=[pl.BlockSpec((None, rows, left.shape[2]), lambda t: (slot, 0, 0)) for left in lefts]
        + [pl.BlockSpec((right.shape[0], tile), lambda t: (0, chunk * tiles + t)) for right in rights],
        out_specs=pl.BlockSpec((rows, tile), lambda t: (0, t)),
        out_shape=jax.ShapeDtypeStruct((rows, columns), dtype),
        cost_estimate=pl.CostEstimate(
            flops=2 * rows * depth * columns,
            bytes_accessed=2 * depth * (columns + rows) + 4 * rows * columns,
            transcendentals=0,
        ),
        name="project",
    )(*lefts, *rights)


def shards(
    query_heads,
    key_heads,
    value_heads,
    residual,
    out_weight,
    mod_weight,
    head_weight,
    latent,
    timesteps,
    token_order,
):
    seq_count = lax.axis_size("seq")
    seq_index = lax.axis_index("seq")
    expert_index = lax.axis_index("expert")
    group_count = lax.axis_size("groups")
    group_bit = lax.axis_index("groups") & 1
    cycle_count = seq_count // DEGREE
    place = seq_index // cycle_count
    cycle = seq_index % cycle_count
    rows = query_heads.shape[2]
    model_width = residual.shape[3]
    stored = out_weight.shape[1]
    width = cycle_count * stored // CHUNKS

    own_weight = out_weight[0]
    rights = [own_weight]
    starts = [cycle * stored]
    for flip in range(1, cycle_count):
        base = (cycle ^ flip) * stored
        if group_count % 2 == 0:
            half = stored // 2
            mine = lax.dynamic_slice_in_dim(own_weight, group_bit * half, half, 0)
            first = swap(mine, "seq", flip)
            second = swap(first, "groups", 1)
            rights += [first, second]
            starts += [base + group_bit * half, base + (1 - group_bit) * half]
        else:
            rights.append(swap(own_weight, "seq", flip))
            starts.append(base)

    orders = lax.dynamic_index_in_dim(token_order, expert_index, 0, keepdims=False)[0]
    own_tokens = lax.dynamic_slice_in_dim(orders, seq_index * rows, rows)
    angles = jnp.repeat(rope_angles(own_tokens), 2, axis=1)
    odd = (jnp.arange(HEAD_DIM) % 2 == 1)[None]
    sine = jnp.sin(angles)
    tables = (jnp.cos(angles), jnp.where(odd, 0.0, -sine), jnp.where(odd, sine, 0.0))
    place_arr = place[None].astype(jnp.int32)

    mixed = []
    for chunk in range(CHUNKS):
        near, far = [], []
        for flip in (3, 2, 1, 0):
            block = turn(
                place_arr, query_heads[0, 0], key_heads[0, 0], value_heads[0, 0], tables, flip, chunk, width
            )
            if flip:
                block = swap(block, "seq", flip * cycle_count)
            near.append(block)
        near = near[::-1]
        for block in near:
            for flip in range(1, cycle_count):
                far.append(swap(block[:2], "seq", flip))
        mixed.append(attend(near, far))
    mixed = jnp.concatenate(mixed, axis=2) if CHUNKS > 1 else mixed[0]
    lefts = [
        lax.dynamic_slice_in_dim(mixed, start, right.shape[0], 2) for start, right in zip(starts, rights)
    ]

    step_value = timesteps[0, 0].astype(jnp.float32)
    embedded = stamp_embedding(step_value).astype(jnp.bfloat16)
    modulation = jnp.dot(embedded[None], mod_weight[0], preferred_element_type=jnp.float32)[0]
    gate_vec = modulation[:model_width]
    shift_vec = modulation[model_width : 2 * model_width]
    scale_vec = modulation[2 * model_width :]

    columns = model_width // COLUMN_CHUNKS
    hidden = []
    for chunk in range(COLUMN_CHUNKS):
        span = slice(chunk * columns, (chunk + 1) * columns)
        far_sum = swap(project(3, chunk, lefts, rights, jnp.bfloat16), "seq", cycle_count)
        near_sum = swap(project(1, chunk, lefts, rights, jnp.bfloat16), "seq", cycle_count)
        passed = project(2, chunk, lefts, rights, jnp.float32) + far_sum.astype(jnp.float32)
        passed = swap(passed.astype(jnp.bfloat16), "seq", 2 * cycle_count)
        kept = project(0, chunk, lefts, rights, jnp.float32) + near_sum.astype(jnp.float32)
        projected = kept + passed.astype(jnp.float32)
        hidden.append(residual[0, 0, :, span].astype(jnp.float32) + gate_vec[span] * projected)
    mean = sum(jnp.sum(part, axis=1, keepdims=True) for part in hidden) / model_width
    centered = [part - mean for part in hidden]
    variance = sum(jnp.sum(part * part, axis=1, keepdims=True) for part in centered) / model_width
    inverse_std = lax.rsqrt(variance + norm_eps)
    velocity = 0.0
    for chunk in range(COLUMN_CHUNKS):
        span = slice(chunk * columns, (chunk + 1) * columns)
        normed = (centered[chunk] * inverse_std * (1.0 + scale_vec[span]) + shift_vec[span]).astype(
            jnp.bfloat16
        )
        velocity += jnp.dot(normed, head_weight[0, span], preferred_element_type=jnp.float32)
    change = noise_level(step_value - STRIDE) - noise_level(step_value)
    stepped = latent[0] + change * velocity
    arrived = swap(stepped.astype(jnp.bfloat16), "expert", 1)[None]
    flip = 1
    positions = seq_index[None]
    while flip < seq_count:
        arrived = jnp.concatenate([arrived, swap(arrived, "seq", flip)], axis=0)
        positions = jnp.concatenate([positions, positions ^ flip])
        flip *= 2
    first_order = token_order[0, 0].reshape(seq_count, rows)[positions].reshape(-1)
    chosen = (own_tokens[:, None] == first_order[None]).astype(jnp.bfloat16)
    started = jnp.dot(
        chosen, arrived.reshape(seq_count * rows, -1), preferred_element_type=jnp.float32
    )
    finished = jnp.where(expert_index == 0, stepped, started + change * velocity)
    return (velocity[None, None], finished[None, None])


def solution(mesh):
    return jax.shard_map(
        shards,
        mesh=mesh,
        in_specs=(
            P("expert", "groups", "seq", None),
            P("expert", "groups", "seq", None),
            P("expert", "groups", "seq", None),
            P("expert", "groups", "seq", None),
            P("expert", "seq", None),
            P("expert", None, None),
            P("expert", None, None),
            P("groups", "seq", None),
            P("expert", "groups"),
            P(None, "groups", None),
        ),
        out_specs=(P("expert", "groups", "seq", None), P("expert", "groups", "seq", None)),
        check_vma=False,
    )
```

```python
import jax
import jax.numpy as jnp
from jax import lax
from jax.experimental import pallas as pl
from jax.experimental.pallas import tpu as pltpu
from jax.sharding import PartitionSpec as P


HEAD_DIM = 128
FREQ = 256
HGRID = 20
WGRID = 52
STRIDE = 25


flow_shift = 5.0
norm_eps = 1e-06

DEGREE = 4
CHUNKS = 4
COLUMN_CHUNKS = 2
LOG2E = 1.4426950408889634


def ladder(length):
    return 10000.0 ** (-jnp.arange(length, dtype=jnp.float32) / length)


def rope_angles(tokens):
    half_dim = HEAD_DIM // 2
    side_pairs = half_dim // 3
    frame_pairs = half_dim - 2 * side_pairs
    frame_pos = (tokens // (HGRID * WGRID)).astype(jnp.float32)
    row_pos = (tokens // WGRID % HGRID).astype(jnp.float32)
    column_pos = (tokens % WGRID).astype(jnp.float32)
    return jnp.concatenate(
        [
            frame_pos[:, None] * ladder(frame_pairs),
            row_pos[:, None] * ladder(side_pairs),
            column_pos[:, None] * ladder(side_pairs),
        ],
        axis=1,
    )


def stamp_embedding(step_value):
    half_freq = FREQ // 2
    inverse_rates = 10000.0 ** (-jnp.arange(half_freq, dtype=jnp.float32) / half_freq)
    phases = step_value * inverse_rates
    return jnp.concatenate([jnp.cos(phases), jnp.sin(phases)])


def noise_level(step_value):
    scaled = step_value / 1000.0
    return flow_shift * scaled / (1.0 + (flow_shift - 1.0) * scaled)


def swap(value, axis, flip):
    return lax.ppermute(value, axis, [(i, i ^ flip) for i in range(lax.axis_size(axis))])


def turn_kernel(place_ref, q_ref, k_ref, v_ref, cos_ref, next_ref, prev_ref, out_ref):
    cosine = cos_ref[...]
    from_next = next_ref[...]
    from_prev = prev_ref[...]

    def turned(field):
        ahead = pltpu.roll(field, HEAD_DIM - 1, 1)
        behind = pltpu.roll(field, 1, 1)
        return field * cosine + ahead * from_next + behind * from_prev

    heads = q_ref.shape[1] // HEAD_DIM
    for head in range(heads):
        cols = pl.ds(head * HEAD_DIM, HEAD_DIM)
        turned_k = turned(k_ref[:, cols].astype(jnp.float32))
        turned_q = turned(q_ref[:, cols].astype(jnp.float32)) * (LOG2E * HEAD_DIM**-0.5)
        out_ref[:, pl.ds(2 * head * HEAD_DIM, HEAD_DIM)] = turned_k.astype(jnp.bfloat16)
        out_ref[:, pl.ds((2 * head + 1) * HEAD_DIM, HEAD_DIM)] = v_ref[:, cols]
        out_ref[:, pl.ds((2 * heads + head) * HEAD_DIM, HEAD_DIM)] = turned_q.astype(jnp.bfloat16)


def turn(place, queries, keys, values, tables, flip, chunk, width):
    rows = queries.shape[0]
    pick = lambda i, place_ref: (0, (place_ref[0] ^ flip) * CHUNKS + chunk)
    fixed = lambda i, place_ref: (0, 0)
    return pl.pallas_call(
        turn_kernel,
        grid_spec=pltpu.PrefetchScalarGridSpec(
            num_scalar_prefetch=1,
            grid=(1,),
            in_specs=[pl.BlockSpec((rows, width), pick)] * 3
            + [pl.BlockSpec((rows, HEAD_DIM), fixed)] * 3,
            out_specs=pl.BlockSpec((rows, 3 * width), fixed),
        ),
        out_shape=jax.ShapeDtypeStruct((rows, 3 * width), jnp.bfloat16),
        cost_estimate=pl.CostEstimate(
            flops=20 * rows * width, bytes_accessed=12 * rows * width, transcendentals=0
        ),
        name="turn",
    )(place, queries, keys, values, *tables)


def attend_kernel(near_count, far_count, padded, *refs):
    pairs = refs[: near_count + far_count]
    asking = refs[near_count + far_count : 2 * near_count + far_count]
    out_ref, k_scr, v_scr = refs[2 * near_count + far_count :]
    rows = pairs[0].shape[0]

    @pl.when(pl.program_id(0) == 0)
    def _():
        k_scr[...] = jnp.zeros_like(k_scr)
        v_scr[...] = jnp.zeros_like(v_scr)

    for slot, block in enumerate(pairs):
        k_scr[pl.ds(slot * padded, rows), :] = block[:, :HEAD_DIM]
        v_scr[pl.ds(slot * padded, rows), :] = block[:, HEAD_DIM:]
    spot = lax.broadcasted_iota(jnp.int32, (1, k_scr.shape[0]), 1) % padded
    hide = jnp.where(spot < rows, 0.0, -1e30).astype(jnp.float32)
    for slot, block in enumerate(asking):
        scores = (
            lax.dot_general(
                block[...], k_scr[...], (((1,), (1,)), ((), ())), preferred_element_type=jnp.float32
            )
            + hide
        )
        top = jnp.max(scores, axis=1, keepdims=True)
        weights = jnp.exp2(scores - top)
        total = jnp.sum(weights, axis=1, keepdims=True)
        mixed = jnp.dot(
            weights.astype(jnp.bfloat16), v_scr[...], preferred_element_type=jnp.float32
        )
        out_ref[slot] = (mixed / total).astype(jnp.bfloat16)


def attend(near, far, width):
    rows = near[0].shape[0]
    padded = -(-rows // 16) * 16
    blocks = len(near) + len(far)
    keys = blocks * padded
    heads = width // HEAD_DIM
    work = len(near) * rows * keys * width
    return pl.pallas_call(
        lambda *refs: attend_kernel(len(near), len(far), padded, *refs),
        grid=(heads,),
        in_specs=[pl.BlockSpec((rows, 2 * HEAD_DIM), lambda h: (0, h))] * blocks
        + [pl.BlockSpec((rows, HEAD_DIM), lambda h: (0, 2 * heads + h))] * len(near),
        out_specs=pl.BlockSpec((len(near), rows, HEAD_DIM), lambda h: (0, 0, h)),
        out_shape=jax.ShapeDtypeStruct((len(near), rows, width), jnp.bfloat16),
        scratch_shapes=[pltpu.VMEM((keys, HEAD_DIM), jnp.bfloat16)] * 2,
        cost_estimate=pl.CostEstimate(
            flops=4 * work, bytes_accessed=8 * blocks * rows * width, transcendentals=work // HEAD_DIM
        ),
        name="attend",
    )(*near, *far, *near)


def project_kernel(count, *refs):
    weight_ref, out_ref = refs[count:]
    total, start = 0.0, 0
    for left in refs[:count]:
        depth = left.shape[1]
        total += jnp.dot(
            left[...], weight_ref[pl.ds(start, depth), :], preferred_element_type=jnp.float32
        )
        start += depth
    out_ref[...] = total.astype(out_ref.dtype)


def project(slot, chunk, lefts, weight, dtype):
    rows = lefts[0].shape[1]
    depth = weight.shape[0]
    columns = weight.shape[1] // COLUMN_CHUNKS
    tiles = 10
    tile = columns // tiles
    return pl.pallas_call(
        lambda *refs: project_kernel(len(lefts), *refs),
        grid=(tiles,),
        in_specs=[pl.BlockSpec((None, rows, left.shape[2]), lambda t: (slot, 0, 0)) for left in lefts]
        + [pl.BlockSpec((depth, tile), lambda t: (0, chunk * tiles + t))],
        out_specs=pl.BlockSpec((rows, tile), lambda t: (0, t)),
        out_shape=jax.ShapeDtypeStruct((rows, columns), dtype),
        cost_estimate=pl.CostEstimate(
            flops=2 * rows * depth * columns,
            bytes_accessed=2 * depth * (columns + rows) + 4 * rows * columns,
            transcendentals=0,
        ),
        name="project",
    )(*lefts, weight)


def shards(
    query_heads,
    key_heads,
    value_heads,
    residual,
    out_weight,
    mod_weight,
    head_weight,
    latent,
    timesteps,
    token_order,
):
    seq_count = lax.axis_size("seq")
    seq_index = lax.axis_index("seq")
    expert_index = lax.axis_index("expert")
    group_count = lax.axis_size("groups")
    group_bit = lax.axis_index("groups") & 1
    cycle_count = seq_count // DEGREE
    place = seq_index // cycle_count
    cycle = seq_index % cycle_count
    rows = query_heads.shape[2]
    model_width = residual.shape[3]
    stored = out_weight.shape[1]
    width = cycle_count * stored // CHUNKS

    own_weight = out_weight[0]
    weight = jnp.zeros((cycle_count * stored, model_width), own_weight.dtype)
    weight = lax.dynamic_update_slice_in_dim(weight, own_weight, cycle * stored, 0)
    for flip in range(1, cycle_count):
        base = (cycle ^ flip) * stored
        if group_count % 2 == 0:
            half = stored // 2
            mine = lax.dynamic_slice_in_dim(own_weight, group_bit * half, half, 0)
            first = swap(mine, "seq", flip)
            second = swap(first, "groups", 1)
            weight = lax.dynamic_update_slice_in_dim(weight, first, base + group_bit * half, 0)
            weight = lax.dynamic_update_slice_in_dim(weight, second, base + (1 - group_bit) * half, 0)
        else:
            weight = lax.dynamic_update_slice_in_dim(weight, swap(own_weight, "seq", flip), base, 0)

    orders = lax.dynamic_index_in_dim(token_order, expert_index, 0, keepdims=False)[0]
    own_tokens = lax.dynamic_slice_in_dim(orders, seq_index * rows, rows)
    angles = jnp.repeat(rope_angles(own_tokens), 2, axis=1)
    odd = (jnp.arange(HEAD_DIM) % 2 == 1)[None]
    sine = jnp.sin(angles)
    tables = (jnp.cos(angles), jnp.where(odd, 0.0, -sine), jnp.where(odd, sine, 0.0))
    place_arr = place[None].astype(jnp.int32)

    mixed = []
    for chunk in range(CHUNKS):
        near, far = [], []
        for flip in (3, 2, 1, 0):
            block = turn(
                place_arr,
                query_heads[0, 0],
                key_heads[0, 0],
                value_heads[0, 0],
                tables,
                flip,
                chunk,
                width,
            )
            if flip:
                block = swap(block, "seq", flip * cycle_count)
            near.append(block)
        near = near[::-1]
        for block in near:
            for flip in range(1, cycle_count):
                far.append(swap(block[:, : 2 * width], "seq", flip))
        mixed.append(attend(near, far, width))

    step_value = timesteps[0, 0].astype(jnp.float32)
    embedded = stamp_embedding(step_value).astype(jnp.bfloat16)
    modulation = jnp.dot(embedded[None], mod_weight[0], preferred_element_type=jnp.float32)[0]
    gate_vec = modulation[:model_width]
    shift_vec = modulation[model_width : 2 * model_width]
    scale_vec = modulation[2 * model_width :]

    columns = model_width // COLUMN_CHUNKS
    hidden = []
    for chunk in range(COLUMN_CHUNKS):
        span = slice(chunk * columns, (chunk + 1) * columns)
        far_sum = swap(project(3, chunk, mixed, weight, jnp.bfloat16), "seq", cycle_count)
        near_sum = swap(project(1, chunk, mixed, weight, jnp.bfloat16), "seq", cycle_count)
        passed = project(2, chunk, mixed, weight, jnp.float32) + far_sum.astype(jnp.float32)
        passed = swap(passed.astype(jnp.bfloat16), "seq", 2 * cycle_count)
        kept = project(0, chunk, mixed, weight, jnp.float32) + near_sum.astype(jnp.float32)
        projected = kept + passed.astype(jnp.float32)
        hidden.append(residual[0, 0, :, span].astype(jnp.float32) + gate_vec[span] * projected)
    mean = sum(jnp.sum(part, axis=1, keepdims=True) for part in hidden) / model_width
    centered = [part - mean for part in hidden]
    variance = sum(jnp.sum(part * part, axis=1, keepdims=True) for part in centered) / model_width
    inverse_std = lax.rsqrt(variance + norm_eps)
    velocity = 0.0
    for chunk in range(COLUMN_CHUNKS):
        span = slice(chunk * columns, (chunk + 1) * columns)
        normed = (centered[chunk] * inverse_std * (1.0 + scale_vec[span]) + shift_vec[span]).astype(
            jnp.bfloat16
        )
        velocity += jnp.dot(normed, head_weight[0, span], preferred_element_type=jnp.float32)
    change = noise_level(step_value - STRIDE) - noise_level(step_value)
    stepped = latent[0] + change * velocity
    arrived = lax.ppermute(stepped.astype(jnp.bfloat16), "expert", [(0, 1)])[None]
    positions = seq_index[None]
    flip = seq_count // 2
    while flip:
        route = [(seq_count + i, seq_count + (i ^ flip)) for i in range(seq_count)]
        arrived = jnp.concatenate([arrived, lax.ppermute(arrived, ("expert", "seq"), route)], axis=0)
        positions = jnp.concatenate([positions, positions ^ flip])
        flip //= 2
    first_order = token_order[0, 0].reshape(seq_count, rows)[positions].reshape(-1)
    chosen = (own_tokens[:, None] == first_order[None]).astype(jnp.bfloat16)
    started = jnp.dot(
        chosen, arrived.reshape(seq_count * rows, -1), preferred_element_type=jnp.float32
    )
    finished = jnp.where(expert_index == 0, stepped, started + change * velocity)
    return (velocity[None, None], finished[None, None])


def solution(mesh):
    return jax.shard_map(
        shards,
        mesh=mesh,
        in_specs=(
            P("expert", "groups", "seq", None),
            P("expert", "groups", "seq", None),
            P("expert", "groups", "seq", None),
            P("expert", "groups", "seq", None),
            P("expert", "seq", None),
            P("expert", None, None),
            P("expert", None, None),
            P("groups", "seq", None),
            P("expert", "groups"),
            P(None, "groups", None),
        ),
        out_specs=(P("expert", "groups", "seq", None), P("expert", "groups", "seq", None)),
        check_vma=False,
    )
```

```python
import jax
import jax.numpy as jnp
from jax import lax
from jax.experimental import pallas as pl
from jax.experimental.pallas import tpu as pltpu
from jax.sharding import PartitionSpec as P


HEAD_DIM = 128
FREQ = 256
HGRID = 20
WGRID = 52
STRIDE = 25


flow_shift = 5.0
norm_eps = 1e-06

DEGREE = 4
CHUNKS = 4
COLUMN_CHUNKS = 2
LOG2E = 1.4426950408889634


def ladder(length):
    return 10000.0 ** (-jnp.arange(length, dtype=jnp.float32) / length)


def rope_angles(tokens):
    half_dim = HEAD_DIM // 2
    side_pairs = half_dim // 3
    frame_pairs = half_dim - 2 * side_pairs
    frame_pos = (tokens // (HGRID * WGRID)).astype(jnp.float32)
    row_pos = (tokens // WGRID % HGRID).astype(jnp.float32)
    column_pos = (tokens % WGRID).astype(jnp.float32)
    return jnp.concatenate(
        [
            frame_pos[:, None] * ladder(frame_pairs),
            row_pos[:, None] * ladder(side_pairs),
            column_pos[:, None] * ladder(side_pairs),
        ],
        axis=1,
    )


def stamp_embedding(step_value):
    half_freq = FREQ // 2
    inverse_rates = 10000.0 ** (-jnp.arange(half_freq, dtype=jnp.float32) / half_freq)
    phases = step_value * inverse_rates
    return jnp.concatenate([jnp.cos(phases), jnp.sin(phases)])


def noise_level(step_value):
    scaled = step_value / 1000.0
    return flow_shift * scaled / (1.0 + (flow_shift - 1.0) * scaled)


def swap(value, axis, flip):
    return lax.ppermute(value, axis, [(i, i ^ flip) for i in range(lax.axis_size(axis))])


def turn_kernel(place_ref, q_ref, k_ref, v_ref, cos_ref, next_ref, prev_ref, out_ref):
    cosine = cos_ref[...]
    from_next = next_ref[...]
    from_prev = prev_ref[...]

    def turned(field):
        ahead = pltpu.roll(field, HEAD_DIM - 1, 1)
        behind = pltpu.roll(field, 1, 1)
        return field * cosine + ahead * from_next + behind * from_prev

    heads = q_ref.shape[1] // HEAD_DIM
    for head in range(heads):
        cols = pl.ds(head * HEAD_DIM, HEAD_DIM)
        turned_k = turned(k_ref[:, cols].astype(jnp.float32))
        turned_q = turned(q_ref[:, cols].astype(jnp.float32)) * (LOG2E * HEAD_DIM**-0.5)
        out_ref[:, pl.ds(2 * head * HEAD_DIM, HEAD_DIM)] = turned_k.astype(jnp.bfloat16)
        out_ref[:, pl.ds((2 * head + 1) * HEAD_DIM, HEAD_DIM)] = v_ref[:, cols]
        out_ref[:, pl.ds((2 * heads + head) * HEAD_DIM, HEAD_DIM)] = turned_q.astype(jnp.bfloat16)


def turn(place, queries, keys, values, tables, flip, chunk, width):
    rows = queries.shape[0]
    pick = lambda i, place_ref: (0, (place_ref[0] ^ flip) * CHUNKS + chunk)
    fixed = lambda i, place_ref: (0, 0)
    return pl.pallas_call(
        turn_kernel,
        grid_spec=pltpu.PrefetchScalarGridSpec(
            num_scalar_prefetch=1,
            grid=(1,),
            in_specs=[pl.BlockSpec((rows, width), pick)] * 3
            + [pl.BlockSpec((rows, HEAD_DIM), fixed)] * 3,
            out_specs=pl.BlockSpec((rows, 3 * width), fixed),
        ),
        out_shape=jax.ShapeDtypeStruct((rows, 3 * width), jnp.bfloat16),
        cost_estimate=pl.CostEstimate(
            flops=20 * rows * width, bytes_accessed=12 * rows * width, transcendentals=0
        ),
        name="turn",
    )(place, queries, keys, values, *tables)


def attend_kernel(near_count, far_count, padded, *refs):
    pairs = refs[: near_count + far_count]
    asking = refs[near_count + far_count : 2 * near_count + far_count]
    out_ref, k_scr, v_scr = refs[-3:]
    rows = pairs[0].shape[0]

    @pl.when(pl.program_id(0) == 0)
    def _():
        k_scr[...] = jnp.zeros_like(k_scr)
        v_scr[...] = jnp.zeros_like(v_scr)

    for slot, block in enumerate(pairs):
        k_scr[pl.ds(slot * padded, rows), :] = block[:, :HEAD_DIM]
        v_scr[pl.ds(slot * padded, rows), :] = block[:, HEAD_DIM:]
    spot = lax.broadcasted_iota(jnp.int32, (1, k_scr.shape[0]), 1) % padded
    hide = jnp.where(spot < rows, 0.0, -1e30).astype(jnp.float32)
    for slot, block in enumerate(asking):
        scores = (
            lax.dot_general(
                block[...], k_scr[...], (((1,), (1,)), ((), ())), preferred_element_type=jnp.float32
            )
            + hide
        )
        top = jnp.max(scores, axis=1, keepdims=True)
        weights = jnp.exp2(scores - top)
        total = jnp.sum(weights, axis=1, keepdims=True)
        mixed = jnp.dot(
            weights.astype(jnp.bfloat16), v_scr[...], preferred_element_type=jnp.float32
        )
        out_ref[slot] = (mixed / total).astype(jnp.bfloat16)


def attend(near, far, width, mixed, chunk):
    rows = near[0].shape[0]
    padded = -(-rows // 16) * 16
    blocks = len(near) + len(far)
    keys = blocks * padded
    heads = width // HEAD_DIM
    work = len(near) * rows * keys * width
    return pl.pallas_call(
        lambda *refs: attend_kernel(len(near), len(far), padded, *refs),
        grid=(heads,),
        in_specs=[pl.BlockSpec((rows, 2 * HEAD_DIM), lambda h: (0, h))] * blocks
        + [pl.BlockSpec((rows, HEAD_DIM), lambda h: (0, 2 * heads + h))] * len(near)
        + [pl.BlockSpec(memory_space=pl.ANY)] * (mixed is not None),
        out_specs=pl.BlockSpec((len(near), rows, HEAD_DIM), lambda h: (0, 0, chunk * heads + h)),
        out_shape=jax.ShapeDtypeStruct((len(near), rows, CHUNKS * width), jnp.bfloat16),
        input_output_aliases={} if mixed is None else {2 * len(near) + len(far): 0},
        scratch_shapes=[pltpu.VMEM((keys, HEAD_DIM), jnp.bfloat16)] * 2,
        cost_estimate=pl.CostEstimate(
            flops=4 * work, bytes_accessed=8 * blocks * rows * width, transcendentals=work // HEAD_DIM
        ),
        name="attend",
    )(*near, *far, *near, *([] if mixed is None else [mixed]))


def project(block, weight, dtype):
    return jnp.dot(block, weight, preferred_element_type=jnp.float32).astype(dtype)


def shards(
    query_heads,
    key_heads,
    value_heads,
    residual,
    out_weight,
    mod_weight,
    head_weight,
    latent,
    timesteps,
    token_order,
):
    seq_count = lax.axis_size("seq")
    seq_index = lax.axis_index("seq")
    expert_index = lax.axis_index("expert")
    group_count = lax.axis_size("groups")
    group_bit = lax.axis_index("groups") & 1
    cycle_count = seq_count // DEGREE
    place = seq_index // cycle_count
    cycle = seq_index % cycle_count
    rows = query_heads.shape[2]
    model_width = residual.shape[3]
    stored = out_weight.shape[1]
    width = cycle_count * stored // CHUNKS

    own_weight = out_weight[0]
    columns = model_width // COLUMN_CHUNKS
    spans = [slice(chunk * columns, (chunk + 1) * columns) for chunk in range(COLUMN_CHUNKS)]
    weights = [jnp.concatenate([own_weight[:, span]] * cycle_count, axis=0) for span in spans]

    def put(piece, start):
        return [
            lax.dynamic_update_slice_in_dim(whole, piece[:, span], start, 0)
            for whole, span in zip(weights, spans)
        ]

    for flip in range(1, cycle_count):
        base = (cycle ^ flip) * stored
        if group_count % 2 == 0:
            half = stored // 2
            mine = lax.dynamic_slice_in_dim(own_weight, group_bit * half, half, 0)
            first = swap(mine, "seq", flip)
            second = swap(first, "groups", 1)
            weights = put(first, base + group_bit * half)
            weights = put(second, base + (1 - group_bit) * half)
        else:
            weights = put(swap(own_weight, "seq", flip), base)

    orders = lax.dynamic_index_in_dim(token_order, expert_index, 0, keepdims=False)[0]
    own_tokens = lax.dynamic_slice_in_dim(orders, seq_index * rows, rows)
    angles = jnp.repeat(rope_angles(own_tokens), 2, axis=1)
    odd = (jnp.arange(HEAD_DIM) % 2 == 1)[None]
    sine = jnp.sin(angles)
    tables = (jnp.cos(angles), jnp.where(odd, 0.0, -sine), jnp.where(odd, sine, 0.0))
    place_arr = place[None].astype(jnp.int32)

    mixed = None
    for chunk in range(CHUNKS):
        near, far = [], []
        for flip in (3, 2, 1, 0):
            block = turn(
                place_arr,
                query_heads[0, 0],
                key_heads[0, 0],
                value_heads[0, 0],
                tables,
                flip,
                chunk,
                width,
            )
            if flip:
                block = swap(block, "seq", flip * cycle_count)
            near.append(block)
        near = near[::-1]
        for block in near:
            for flip in range(1, cycle_count):
                far.append(swap(block[:, : 2 * width], "seq", flip))
        mixed = attend(near, far, width, mixed, chunk)

    step_value = timesteps[0, 0].astype(jnp.float32)
    embedded = stamp_embedding(step_value).astype(jnp.bfloat16)
    modulation = jnp.dot(embedded[None], mod_weight[0], preferred_element_type=jnp.float32)[0]
    gate_vec = modulation[:model_width]
    shift_vec = modulation[model_width : 2 * model_width]
    scale_vec = modulation[2 * model_width :]

    hidden = []
    for chunk in range(COLUMN_CHUNKS):
        span = slice(chunk * columns, (chunk + 1) * columns)
        far_sum = swap(project(mixed[3], weights[chunk], jnp.bfloat16), "seq", cycle_count)
        near_sum = swap(project(mixed[1], weights[chunk], jnp.bfloat16), "seq", cycle_count)
        passed = project(mixed[2], weights[chunk], jnp.float32) + far_sum.astype(jnp.float32)
        passed = swap(passed.astype(jnp.bfloat16), "seq", 2 * cycle_count)
        kept = lax.optimization_barrier(project(mixed[0], weights[chunk], jnp.float32))
        kept += near_sum.astype(jnp.float32)
        projected = kept + passed.astype(jnp.float32)
        hidden.append(residual[0, 0, :, span].astype(jnp.float32) + gate_vec[span] * projected)
    mean = sum(jnp.sum(part, axis=1, keepdims=True) for part in hidden) / model_width
    centered = [part - mean for part in hidden]
    variance = sum(jnp.sum(part * part, axis=1, keepdims=True) for part in centered) / model_width
    inverse_std = lax.rsqrt(variance + norm_eps)
    velocity = 0.0
    for chunk in range(COLUMN_CHUNKS):
        span = slice(chunk * columns, (chunk + 1) * columns)
        normed = (centered[chunk] * inverse_std * (1.0 + scale_vec[span]) + shift_vec[span]).astype(
            jnp.bfloat16
        )
        velocity += jnp.dot(normed, head_weight[0, span], preferred_element_type=jnp.float32)
    change = noise_level(step_value - STRIDE) - noise_level(step_value)
    stepped = latent[0] + change * velocity
    sent = stepped.astype(jnp.bfloat16)
    arrived = []
    for flip in range(seq_count - 1, -1, -1):
        route = [(i, seq_count + (i ^ flip)) for i in range(seq_count)]
        arrived.append(lax.ppermute(sent, ("expert", "seq"), route))
    positions = jnp.stack([seq_index ^ flip for flip in range(seq_count - 1, -1, -1)])
    first_order = token_order[0, 0].reshape(seq_count, rows)[positions].reshape(-1)
    chosen = (own_tokens[:, None] == first_order[None]).astype(jnp.bfloat16)
    started = jnp.dot(chosen, jnp.concatenate(arrived), preferred_element_type=jnp.float32)
    finished = jnp.where(expert_index == 0, stepped, started + change * velocity)
    return (velocity[None, None], finished[None, None])


def solution(mesh):
    return jax.shard_map(
        shards,
        mesh=mesh,
        in_specs=(
            P("expert", "groups", "seq", None),
            P("expert", "groups", "seq", None),
            P("expert", "groups", "seq", None),
            P("expert", "groups", "seq", None),
            P("expert", "seq", None),
            P("expert", None, None),
            P("expert", None, None),
            P("groups", "seq", None),
            P("expert", "groups"),
            P(None, "groups", None),
        ),
        out_specs=(P("expert", "groups", "seq", None), P("expert", "groups", "seq", None)),
        check_vma=False,
    )
```
